128 devices in a mesh: dp: 8 (over z, core), expert: 16 (over x, y).
Axes of the slice: x: 4, y: 4, z: 4, core: 2. Of those that a mesh axis runs over, the one named last changes fastest.
Arguments:
- tokens: bfloat16 [16384, 2048], P(('dp', 'expert')), may hold values from -6 to 6
- cotangent: bfloat16 [16384, 2048], P(('dp', 'expert')), may hold values from -6 to 6
- expert_ids: int32 [16384, 8], P(('dp', 'expert')), may hold values from 0 to 63, as said below
- slot_ids: int32 [16384, 8], P(('dp', 'expert')), may hold values from 0 to 19, as said below
- gate_weights: float32 [16384, 8], P(('dp', 'expert')), may hold values from 0.03 to 0.5
- w_gate_up: bfloat16 [64, 2048, 768], P('expert', 'dp'), may hold values from -0.125 to 0.125
- w_down: bfloat16 [64, 384, 2048], P('expert', None, 'dp'), may hold values from -0.3125 to 0.3125
Outputs:
- mixed: bfloat16 [16384, 2048], P(('dp', 'expert'))
- tokens_grad: bfloat16 [16384, 2048], P(('dp', 'expert'))
The draws below stay inside these ranges and needn't reach their ends.
Inputs may be any that keep to these rules, and one draw needn't show every extreme that they name: `expert_ids`: each row names 8 different experts. In the rows of one device (aligned blocks of 128 rows) no expert is named by more than 20 rows; in every such block some expert is named by exactly 20 rows, and one expert is named by 20 rows in every block. Among the rows of one device that name one expert, slot_ids at that expert are distinct and run from 0 to their number minus one.
All inputs are finite; a program needn't handle non-finite values.
Results may differ from the reference program's by a relative error of at most 0.0064.
Values may be sent and summed in bfloat16 or wider, within the bound.
No kernel may reach another device: no remote copies, remote signals or barrier semaphores. Data moves between devices by JAX's collectives and lax.ppermute only.
A program may use at most 128 MiB of HBM per device.

```python
import math
import jax
import jax.numpy as jnp
from jax import lax

D = 2048
H = 384
TOPK = 8
T_DEV = 128
E = 64
TOKENS = 16384
CAP = 20


def routing_table(key):
    blocks = TOKENS // T_DEV
    mean_load = T_DEV * TOPK // E
    spare = CAP - mean_load
    base = jax.random.fold_in(key, 911)
    key_star, key_perm, key_shift, key_rows, key_cols = jax.random.split(base, 5)
    hot_expert = jax.random.randint(key_star, (), 0, E, dtype=jnp.int32)
    orders = jax.vmap(lambda sub: jax.random.permutation(sub, E))(jax.random.split(key_perm, blocks)).astype(jnp.int32)
    leading = orders[:, :1]
    orders = jnp.where(orders == hot_expert, leading, orders)
    orders = orders.at[:, 0].set(hot_expert)
    shifts = jax.random.randint(key_shift, (blocks, E // 2), 0, spare + 1, dtype=jnp.int32)
    shifts = shifts.at[:, 0].set(spare)
    by_position = jnp.stack([mean_load + shifts, mean_load - shifts], axis=-1).reshape(blocks, E)
    block_index = jnp.arange(blocks, dtype=jnp.int32)[:, None]
    counts = jnp.zeros((blocks, E), jnp.int32).at[block_index, orders].set(by_position)
    ends = jnp.cumsum(counts, axis=1).astype(jnp.int32)
    starts = ends - counts
    places = jnp.arange(T_DEV * TOPK, dtype=jnp.int32)
    owner = jnp.sum((ends[:, None, :] <= places[None, :, None]).astype(jnp.int32), axis=2).astype(jnp.int32)
    rank = places[None, :] - jnp.take_along_axis(starts, owner, axis=1)
    owner = owner.reshape(blocks, TOPK, T_DEV).transpose(0, 2, 1)
    rank = rank.reshape(blocks, TOPK, T_DEV).transpose(0, 2, 1)
    row_orders = jax.vmap(lambda sub: jax.random.permutation(sub, T_DEV))(jax.random.split(key_rows, blocks)).astype(jnp.int32)
    owner = jnp.take_along_axis(owner, row_orders[:, :, None], axis=1)
    rank = jnp.take_along_axis(rank, row_orders[:, :, None], axis=1)
    col_orders = jax.vmap(lambda sub: jax.random.permutation(sub, TOPK))(jax.random.split(key_cols, blocks * T_DEV)).astype(jnp.int32)
    col_orders = col_orders.reshape(blocks, T_DEV, TOPK)
    owner = jnp.take_along_axis(owner, col_orders, axis=2)
    rank = jnp.take_along_axis(rank, col_orders, axis=2)
    return (owner.reshape(TOKENS, TOPK).astype(jnp.int32), rank.reshape(TOKENS, TOPK).astype(jnp.int32))


def draw_expert_ids(key, part):
    chosen, placed = routing_table(key)
    return chosen


def draw_slot_ids(key, part):
    chosen, placed = routing_table(key)
    return placed


def levels(own_key, dims, shards, least, high):
    def one(dim, blocks):
        steps = jax.random.uniform(jax.random.fold_in(jax.random.fold_in(own_key, 6), dim), (blocks,), jnp.float32, least / len(shards), high / len(shards))
        return jnp.repeat(jnp.exp(steps), dims[dim] // blocks).reshape((-1,) + (1,) * (len(dims) - dim - 1))

    gain = one(*shards[0])
    for cut in shards[1:]:
        gain = gain * one(*cut)
    return gain


def normal_values(own_key, extent, deviation, most, shards=(), kind=jnp.bfloat16):
    entries = deviation * jax.random.normal(own_key, extent, jnp.float32)
    if shards:
        entries = entries * levels(own_key, extent, shards, -0.22, 0.18)
    return jnp.clip(entries, -most, most).astype(kind)


def setup_inputs(seed: int = 0) -> dict:
    splits = jax.random.split(jax.random.key(seed), 8)
    tokens = normal_values(splits[0], (TOKENS, D), 1.0, 6.0, ((0, 128),))
    cotangent = normal_values(splits[1], (TOKENS, D), 1.0, 6.0, ((0, 128),))
    expert_ids = draw_expert_ids(jax.random.fold_in(splits[7], 71), 0)
    slot_ids = draw_slot_ids(jax.random.fold_in(splits[7], 71), 0)
    gate_weights = jnp.clip(jnp.exp(math.log(0.5) - 2.8134107 * jax.random.uniform(splits[4], (TOKENS, TOPK), jnp.float32) ** levels(splits[4], (TOKENS, TOPK), ((0, 128),), -0.2, 0.2)), 0.03, 0.5)
    w_gate_up = normal_values(splits[5], (E, D, 2 * H), D ** -0.5, 0.125, ((0, 16), (1, 8)))
    w_down = normal_values(splits[6], (E, H, D), H ** -0.5, 0.3125, ((0, 16), (2, 8)))
    return {"tokens": tokens, "cotangent": cotangent, "expert_ids": expert_ids, "slot_ids": slot_ids, "gate_weights": gate_weights, "w_gate_up": w_gate_up, "w_down": w_down}


def reference(tokens, cotangent, expert_ids, slot_ids, gate_weights, w_gate_up, w_down):
    tok_total = tokens.shape[0]
    width = tokens.shape[1]
    per_expert = (tok_total // T_DEV) * CAP
    tok_index = jnp.arange(tok_total, dtype=jnp.int32)
    source = tok_index // T_DEV
    places = (expert_ids * per_expert + source[:, None] * CAP + slot_ids).astype(jnp.int32).reshape(-1)
    owners = jnp.full((E * per_expert,), tok_total, jnp.int32)
    owners = owners.at[places].set(jnp.broadcast_to(tok_index[:, None], expert_ids.shape).reshape(-1))
    weighting = jnp.zeros((E * per_expert,), jnp.float32).at[places].set(gate_weights.reshape(-1))
    owners = owners.reshape(E, per_expert)
    weighting = weighting.reshape(E, per_expert)
    padding = jnp.zeros((1, width), tokens.dtype)
    tokens_pad = jnp.concatenate([tokens, padding], axis=0)
    cotangent_pad = jnp.concatenate([cotangent, padding], axis=0)

    def one_expert(running, inputs):
        mixed_acc, grad_acc = running
        gate_up, down, rows, weights_here = inputs
        gate_up32 = gate_up.astype(jnp.float32)
        down32 = down.astype(jnp.float32)
        rows_in = tokens_pad[rows].astype(jnp.float32)
        preact = jnp.dot(rows_in, gate_up32)
        gate_part = preact[:, :H]
        up_part = preact[:, H:]
        hidden_act = (jax.nn.silu(gate_part) * up_part).astype(jnp.bfloat16)
        expert_out = jnp.dot(hidden_act.astype(jnp.float32), down32).astype(jnp.bfloat16)
        mixed_acc = mixed_acc.at[rows].add(weights_here[:, None] * expert_out.astype(jnp.float32), mode="drop")
        scaled = (weights_here[:, None] * cotangent_pad[rows].astype(jnp.float32)).astype(jnp.bfloat16)
        grad_hidden = jnp.dot(scaled.astype(jnp.float32), down32.T)
        sigmoid_gate = jax.nn.sigmoid(gate_part)
        grad_gate = grad_hidden * up_part * sigmoid_gate * (1.0 + gate_part * (1.0 - sigmoid_gate))
        grad_up = grad_hidden * (gate_part * sigmoid_gate)
        grad_pre = jnp.concatenate([grad_gate, grad_up], axis=1).astype(jnp.bfloat16)
        grad_choice = jnp.dot(grad_pre.astype(jnp.float32), gate_up32.T).astype(jnp.bfloat16)
        grad_acc = grad_acc.at[rows].add(grad_choice.astype(jnp.float32), mode="drop")
        return (mixed_acc, grad_acc), None

    start_acc = (jnp.zeros((tok_total, width), jnp.float32), jnp.zeros((tok_total, width), jnp.float32))
    (mixed_acc, grad_acc), unused = lax.scan(one_expert, start_acc, (w_gate_up, w_down, owners, weighting))
    return mixed_acc.astype(jnp.bfloat16), grad_acc.astype(jnp.bfloat16)
```

```python
import jax
import jax.numpy as jnp
from jax import lax
from jax.sharding import PartitionSpec as P

F32 = jnp.float32
BF16 = jnp.bfloat16


def torus_side(count):
    side = 1
    while side * side < count:
        side += 1
    return side


def hop(value, along, step):
    side = torus_side(lax.axis_size("expert"))
    pairs = []
    for x in range(side):
        for y in range(side):
            to = ((x + step) % side, y) if along == "x" else (x, (y + step) % side)
            pairs.append((x * side + y, to[0] * side + to[1]))
    return lax.ppermute(value, "expert", pairs)


def ring_gather(own, along):
    half = own.shape[0] // 2
    before = hop(own, along, 1)
    after = hop(own, along, -1)
    far = [hop(before[:half], along, 1), hop(after[half:], along, -1)]
    return jnp.stack([own, before, after, jnp.concatenate(far, axis=0)])


def torus_gather(rows, first, second):
    return ring_gather(ring_gather(rows, first), second)


def ring_scatter(parts):
    def run(parts, along):
        own, back, ahead, far = parts
        half = own.shape[0] // 2
        from_back = hop(far[:half], along, 1)
        from_ahead = hop(far[half:], along, -1)
        plain_up = hop(ahead[half:], along, 1)
        plain_down = hop(back[:half], along, -1)
        add = lambda *terms: sum(t.astype(F32) for t in terms).astype(BF16)
        up = hop(add(ahead[:half], from_back), along, 1)
        down = hop(add(back[half:], from_ahead), along, -1)
        low = add(own[:half], up, plain_down)
        high = add(own[half:], plain_up, down)
        return jnp.concatenate([low, high], axis=0)

    return run


def torus_scatter(parts, first, second):
    run = ring_scatter(None)
    return run(run(parts, first), second)


def small_gather(value):
    for along in ("x", "y"):
        value = jnp.concatenate([value, hop(value, along, 1)], axis=0)
        value = jnp.concatenate([value, hop(value, along, 2)], axis=0)
    return value


def body(tokens, cotangent, expert_ids, slot_ids, gate_weights, w_gate_up, w_down):
    tok_count, model_width = tokens.shape
    top_count = expert_ids.shape[1]
    local_experts = w_gate_up.shape[0]
    hidden_width = w_down.shape[1]
    group = lax.axis_size("expert")
    expert_total = local_experts * group
    capacity = 5 * tok_count * top_count // (4 * expert_total)
    local_rows = local_experts * capacity
    half = tok_count // 2

    places = (expert_ids * capacity + slot_ids).astype(F32).T
    info = small_gather(jnp.concatenate([places, gate_weights.T], axis=0)[None])
    info = info.reshape(4, 4, 2 * top_count, tok_count)
    order = jnp.array([0, 1, 3, 2])
    info = info[order][:, order]
    base = (lax.axis_index("expert") * local_rows).astype(F32)
    wanted = base + jnp.arange(local_rows, dtype=F32)[:, None]
    hit = info[:, :, :top_count, None, :] == wanted
    pick = jnp.any(hit, axis=2).astype(BF16)
    row_gate = jnp.sum(jnp.where(hit, info[:, :, top_count:, None, :], 0.0), axis=(2, 4))

    gate_up_full = lax.all_gather(w_gate_up, "dp", axis=1, tiled=True)
    down_full = lax.all_gather(w_down, "dp", axis=2, tiled=True)

    def gathered(rows):
        low = torus_gather(rows[:half], "x", "y")
        high = torus_gather(rows[half:], "y", "x")
        high = jnp.swapaxes(high, 0, 1)
        return jnp.concatenate([low, high], axis=2)

    def scattered(parts):
        low = torus_scatter(parts[:, :, :half], "y", "x")
        high = torus_scatter(jnp.swapaxes(parts[:, :, half:], 0, 1), "x", "y")
        return jnp.concatenate([low, high], axis=0)

    def picked(rows):
        out = jnp.einsum("yxrt,yxtd->yxrd", pick, rows, preferred_element_type=F32).astype(BF16)
        return out.reshape(group, local_experts, capacity, model_width)

    def combined(rows):
        rows = rows.reshape(4, 4, local_rows, model_width)
        return jnp.einsum("yxrt,yxrd->yxtd", pick, rows, preferred_element_type=F32).astype(BF16)

    gate_of = row_gate.reshape(group, local_experts, capacity, 1)
    rows_in = picked(gathered(tokens))
    preact = jnp.einsum("sjcd,jdf->sjcf", rows_in, gate_up_full, preferred_element_type=F32)
    gate_part = preact[..., :hidden_width]
    up_part = preact[..., hidden_width:]
    sigmoid_gate = jax.nn.sigmoid(gate_part)
    hidden_act = (gate_of * (gate_part * sigmoid_gate) * up_part).astype(BF16)
    expert_out = jnp.einsum("sjch,jhd->sjcd", hidden_act, down_full, preferred_element_type=F32)
    mixed = scattered(combined(expert_out.astype(BF16)))

    grads_in = picked(gathered(cotangent))
    grad_hidden = gate_of * jnp.einsum("sjcd,jhd->sjch", grads_in, down_full, preferred_element_type=F32)
    grad_gate = grad_hidden * up_part * sigmoid_gate * (1.0 + gate_part * (1.0 - sigmoid_gate))
    grad_up = grad_hidden * (gate_part * sigmoid_gate)
    grad_pre = jnp.concatenate([grad_gate, grad_up], axis=-1).astype(BF16)
    grad_choice = jnp.einsum("sjcf,jdf->sjcd", grad_pre, gate_up_full, preferred_element_type=F32)
    tokens_grad = scattered(combined(grad_choice.astype(BF16)))
    return (mixed, tokens_grad)


def solution(mesh):
    rows = P(("dp", "expert"), None)
    placed = (rows, rows, rows, rows, rows, P("expert", "dp", None), P("expert", None, "dp"))
    return jax.shard_map(
        body, mesh=mesh, in_specs=placed, out_specs=(rows, rows), check_vma=False
    )
```

```python
import functools

import jax
import jax.numpy as jnp
from jax import lax
from jax.experimental import pallas as pl
from jax.experimental.pallas import tpu as pltpu
from jax.sharding import PartitionSpec as P

F32 = jnp.float32
BF16 = jnp.bfloat16
ANY = pl.BlockSpec(memory_space=pl.ANY)
VMEM = pl.BlockSpec(memory_space=pltpu.VMEM)
SMEM = pl.BlockSpec(memory_space=pltpu.SMEM)
QUADS = ((0, 0), (0, 1), (1, 0), (1, 1))


def hop(value, along, step):
    side = 4
    pairs = []
    for x in range(side):
        for y in range(side):
            to = ((x + step) % side, y) if along == "x" else (x, (y + step) % side)
            pairs.append((x * side + y, to[0] * side + to[1]))
    return lax.ppermute(value, "expert", pairs)


def shift(value, step):
    count = lax.axis_size("dp")
    return lax.ppermute(value, "dp", [(i, (i + 2 * step) % count) for i in range(count)])


def swap(value):
    return lax.ppermute(value, "dp", [(i, i ^ 1) for i in range(lax.axis_size("dp"))])


def ring_gather(own, along):
    half = own.shape[0] // 2
    before = hop(own, along, 1)
    after = hop(own, along, -1)
    far_low = hop(before[:half], along, 1)
    far_high = hop(after[half:], along, -1)
    return own, before, after, far_low, far_high


def torus_gather(rows, first, second):
    own, before, after, low, high = ring_gather(rows, first)
    line = jnp.stack([own, before, after, jnp.concatenate([low, high], axis=0)])
    return ring_gather(line, second)


def z_gather(piece):
    half = piece.shape[0] // 2
    before = shift(piece, 1)
    after = shift(piece, -1)
    pieces = [piece, before, after, shift(before[:half], 1), shift(after[half:], -1)]
    return pieces + [swap(p) for p in pieces]


def add(*terms):
    return sum(t.astype(F32) for t in terms).astype(BF16)


def ring_scatter(own, back, ahead, far, along):
    from_back = hop(far[0], along, 1)
    from_ahead = hop(far[1], along, -1)
    plain_up = hop(ahead[1], along, 1)
    plain_down = hop(back[0], along, -1)
    up = hop(add(ahead[0], from_back), along, 1)
    down = hop(add(back[1], from_ahead), along, -1)
    return add(own[0], up, plain_down), add(own[1], plain_up, down)


def torus_scatter(parts, first, second):
    low, high = ring_scatter(*parts, first)
    half = low.shape[1] // 2
    cut = [(v[i, :half], v[i, half:]) for v in (low, high) for i in (0, 1)]
    return jnp.concatenate(ring_scatter(*cut, second), axis=0)


def small_gather(value):
    for along in ("x", "y"):
        value = jnp.concatenate([value, hop(value, along, 1)], axis=0)
        value = jnp.concatenate([value, hop(value, along, 2)], axis=0)
    return value


def token_copies(refs, buf, sems):
    low, high = refs[:5], refs[5:]
    quads = []
    for q, (qy, qx) in enumerate(QUADS):
        copies = []
        for part, (src, outer, inner) in enumerate(((low, qy, qx), (high, qx, qy))):
            for i in range(2):
                at = 2 * outer + i
                ref = src[3 + inner] if at == 3 else src[at].at[pl.ds(2 * inner, 2)]
                n = part * 2 + i
                copies.append(
                    pltpu.make_async_copy(ref, buf.at[q, pl.ds(2 * n, 2)], sems.at[4 * q + n])
                )
        quads.append(copies)
    return quads


def piece_copies(pos_ref, refs, buf, sems, axis, width):
    me = pos_ref[0]
    core = lax.rem(me, 2)
    out = []
    for n, ref in enumerate(refs):
        k = n % 5
        chip = lax.rem(lax.div(me, 2) + (0, 3, 1, 2, 2)[k], 4)
        at = 2 * chip + (core if n < 5 else 1 - core)
        where = pl.ds(pl.multiple_of(at * width, width), width)
        count = ref.shape[0]
        experts = pl.ds(count if k == 4 else 0, count)
        dst = buf.at[experts, where, :] if axis == 1 else buf.at[experts, :, where]
        out.append(pltpu.make_async_copy(ref, dst, sems.at[n]))
    return out


def pick_kernel(row_ref, rowt_ref, gate_ref, pick_ref, pickt_ref, rowgate_ref):
    rows, tokens = pick_ref.shape[1:]
    per = rows // 4
    top = row_ref.shape[1]

    def quad(q, carry):
        down = lax.broadcasted_iota(jnp.int32, (rows, tokens), 0)
        hits = jnp.zeros((rows, tokens), F32)
        gates = jnp.zeros((rows, tokens), F32)
        for k in range(top):
            same = down == row_ref[q, k : k + 1, :]
            hits = jnp.where(same, 1.0, hits)
            gates = jnp.where(same, gate_ref[q, k : k + 1, :], gates)
        pick_ref[q] = hits.astype(BF16)
        sums = jnp.sum(gates, axis=1, keepdims=True)
        for j in range(4):
            rowgate_ref[j, q] = jnp.broadcast_to(sums[j * per : (j + 1) * per], (per, 128))
        across = lax.broadcasted_iota(jnp.int32, (tokens, rows), 1)
        hits = jnp.zeros((tokens, rows), F32)
        for k in range(top):
            hits = jnp.where(across == rowt_ref[q, :, k : k + 1], 1.0, hits)
        pickt_ref[q] = hits.astype(BF16)
        return carry

    lax.fori_loop(0, 4, quad, 0)


def gather_rows(q, pick_ref, buf, rows_buf):
    width = buf.shape[-1]
    per = pick_ref.shape[1] // 4
    tile = 512

    def column(c, carry):
        at = pl.ds(pl.multiple_of(c * tile, tile), tile)
        tokens = buf[q, :, :, at].reshape(-1, tile)
        rows = jnp.dot(pick_ref[q], tokens, preferred_element_type=F32).astype(BF16)
        for j in range(4):
            rows_buf[j, q * per : (q + 1) * per, at] = rows[j * per : (j + 1) * per]
        return carry

    lax.fori_loop(0, width // tile, column, 0)


def spread_rows(j, values, at, out_rows):
    per = values.shape[0] // 4
    for q in range(4):
        out_rows[q, pl.ds(pl.multiple_of(j * per, 16), per), at] = values[q * per : (q + 1) * per]


def combine_rows(q, pickt_ref, out_rows, buf):
    width = buf.shape[-1]
    tile = 512

    def column(c, carry):
        at = pl.ds(pl.multiple_of(c * tile, tile), tile)
        sums = jnp.dot(pickt_ref[q], out_rows[q, :, at], preferred_element_type=F32)
        buf[q, :, :, at] = sums.astype(BF16).reshape(8, -1, tile)
        return carry

    lax.fori_loop(0, width // tile, column, 0)


def part_copies(q, buf, outs, sems):
    qy, qx = QUADS[q]
    copies = []
    for part, (outer, inner) in enumerate(((qy, qx), (qx, qy))):
        for i in range(2):
            n = part * 2 + i
            ref = outs[part * 8 + (2 * outer + i) * 2 + inner]
            copies.append(
                pltpu.make_async_copy(buf.at[q, pl.ds(2 * n, 2)], ref, sems.at[4 * q + n])
            )
    return copies


def forward_kernel(pos_ref, pick_ref, rowgate_ref, *refs):
    token_refs, weight_refs = refs[:10], refs[10:20]
    pre_ref, hidden_ref, buf, rows_buf, weight, token_sems, weight_sems = refs[20:]
    hid = hidden_ref.shape[-1]
    quads = token_copies(token_refs, buf, token_sems)
    for copies in quads:
        for c in copies:
            c.start()
    weights = piece_copies(pos_ref, weight_refs, weight, weight_sems, 1, weight_refs[0].shape[1])
    for c in weights:
        c.start()
    for q, copies in enumerate(quads):
        for c in copies:
            c.wait()
        gather_rows(q, pick_ref, buf, rows_buf)
    for c in weights:
        c.wait()

    def expert(j, carry):
        pre = jnp.dot(rows_buf[j], weight[j], preferred_element_type=F32)
        pre_ref[j] = pre
        g, u = pre[:, :hid], pre[:, hid:]
        gate = rowgate_ref[j].reshape(-1, 128)[:, :1]
        hidden_ref[j] = (gate * (g / (1.0 + jnp.exp(-g)) * u)).astype(BF16)
        return carry

    lax.fori_loop(0, 4, expert, 0)


def output_kernel(pos_ref, hidden_ref, pickt_ref, *refs):
    weight_refs, outs = refs[:10], refs[10:26]
    buf, out_rows, weight, weight_sems, out_sems = refs[26:]
    tile = 512
    weights = piece_copies(pos_ref, weight_refs, weight, weight_sems, 2, weight_refs[0].shape[2])
    for c in weights:
        c.start()
    for c in weights:
        c.wait()

    def expert(j, carry):
        def column(c, inner):
            at = pl.ds(pl.multiple_of(c * tile, tile), tile)
            out = jnp.dot(hidden_ref[j], weight[j, :, at], preferred_element_type=F32)
            spread_rows(j, out.astype(BF16), at, out_rows)
            return inner

        return lax.fori_loop(0, weight.shape[2] // tile, column, carry)

    lax.fori_loop(0, 4, expert, 0)
    copies = []
    for q in (3, 2, 1, 0):
        combine_rows(q, pickt_ref, out_rows, buf)
        for c in part_copies(q, buf, outs, out_sems):
            c.start()
            copies.append(c)
    for c in copies:
        c.wait()


def backward_kernel(pos_ref, pick_ref, pickt_ref, rowgate_ref, pre_ref, *refs):
    token_refs, up_refs, down_refs, outs = refs[:10], refs[10:20], refs[20:30], refs[30:46]
    buf, rows_buf, out_rows, up_weight, down_weight, grad = refs[46:52]
    token_sems, up_sems, down_sems, out_sems = refs[52:]
    hid = down_weight.shape[1]
    tile = 512
    quads = token_copies(token_refs, buf, token_sems)
    for copies in quads:
        for c in copies:
            c.start()
    downs = piece_copies(pos_ref, down_refs, down_weight, down_sems, 2, down_refs[0].shape[2])
    ups = piece_copies(pos_ref, up_refs, up_weight, up_sems, 1, up_refs[0].shape[1])
    for c in downs + ups:
        c.start()
    for q, copies in enumerate(quads):
        for c in copies:
            c.wait()
        gather_rows(q, pick_ref, buf, rows_buf)
    for c in downs:
        c.wait()
    for c in ups:
        c.wait()
    nt = (((1,), (1,)), ((), ()))

    def expert(j, carry):
        back = lax.dot_general(rows_buf[j], down_weight[j], nt, preferred_element_type=F32)
        back = back * rowgate_ref[j].reshape(-1, 128)[:, :1]
        g, u = pre_ref[j, :, :hid], pre_ref[j, :, hid:]
        s = 1.0 / (1.0 + jnp.exp(-g))
        grad[:, :hid] = (back * u * s * (1.0 + g * (1.0 - s))).astype(BF16)
        grad[:, hid:] = (back * (g * s)).astype(BF16)

        def column(c, inner):
            at = pl.ds(pl.multiple_of(c * tile, tile), tile)
            out = lax.dot_general(
                grad[...], up_weight[j, at, :], nt, preferred_element_type=F32
            )
            spread_rows(j, out.astype(BF16), at, out_rows)
            return inner

        return lax.fori_loop(0, up_weight.shape[1] // tile, column, carry)

    lax.fori_loop(0, 4, expert, 0)
    copies = []
    for q in (3, 2, 1, 0):
        combine_rows(q, pickt_ref, out_rows, buf)
        for c in part_copies(q, buf, outs, out_sems):
            c.start()
            copies.append(c)
    for c in copies:
        c.wait()


def cost(flops, moved):
    return pl.CostEstimate(flops=flops, bytes_accessed=moved, transcendentals=0)


PARAMS = pltpu.CompilerParams(vmem_limit_bytes=60 * 1024 * 1024)
DMA = pltpu.SemaphoreType.DMA


def body(tokens, cotangent, expert_ids, slot_ids, gate_weights, w_gate_up, w_down):
    tok_count, width = tokens.shape
    top = expert_ids.shape[1]
    experts = w_gate_up.shape[0]
    hid = w_down.shape[1]
    group = lax.axis_size("expert")
    capacity = 5 * tok_count * top // (4 * experts * group)
    local_rows = experts * capacity
    half = tok_count // 2
    quad_tokens = 4 * tok_count
    quad_rows = 4 * local_rows
    sds = jax.ShapeDtypeStruct

    places = (expert_ids * capacity + slot_ids).astype(F32).T
    info = small_gather(jnp.concatenate([places, gate_weights.T], axis=0)[None])
    info = info.reshape(4, 4, 2 * top, 2, half)
    info = jnp.stack([info[0], info[1], info[3], info[2]])
    info = jnp.stack([info[:, 0], info[:, 1], info[:, 3], info[:, 2]], axis=1)
    info = info.reshape(2, 2, 2, 2, 2 * top, 2, half)
    owner = (2 * jnp.arange(2)[:, None] + jnp.arange(2))[None, :, None, :, None, None, None]
    place = info[:, :, :, :, :top].astype(jnp.int32) - lax.axis_index("expert") * local_rows
    mine = (place >= 0) & (place < local_rows)
    row = place // capacity * (4 * capacity) + owner * capacity + place % capacity
    row = jnp.where(mine, row, -1)

    def by_quad(v):
        low = v[..., 0, :].transpose(0, 2, 4, 1, 3, 5).reshape(4, top, 2 * tok_count)
        high = v[..., 1, :].transpose(0, 2, 4, 3, 1, 5).reshape(4, top, 2 * tok_count)
        return jnp.concatenate([low, high], axis=2)

    row = by_quad(row)
    gates = by_quad(info[:, :, :, :, top:])
    pick, pickt, rowgate = pl.pallas_call(
        pick_kernel,
        out_shape=(
            sds((4, quad_rows, quad_tokens), BF16),
            sds((4, quad_tokens, quad_rows), BF16),
            sds((experts, 4, quad_rows // 4, 128), F32),
        ),
        in_specs=[VMEM] * 3,
        out_specs=(VMEM,) * 3,
        compiler_params=PARAMS,
        cost_estimate=cost(0, 8 << 20),
    )(row, jnp.swapaxes(row, 1, 2), gates)

    pos = lax.axis_index("dp").astype(jnp.int32).reshape(1)
    ups = z_gather(w_gate_up)
    downs = z_gather(w_down)

    def gathered(rows):
        return torus_gather(rows[:half], "x", "y") + torus_gather(rows[half:], "y", "x")

    def scattered(parts):
        pairs = [(parts[2 * i], parts[2 * i + 1]) for i in range(8)]
        return jnp.concatenate(
            [torus_scatter(pairs[:4], "y", "x"), torus_scatter(pairs[4:], "x", "y")], axis=0
        )

    token_buf = pltpu.VMEM((4, 8, half, width), BF16)
    row_buf = pltpu.VMEM((experts, quad_rows, width), BF16)
    up_buf = pltpu.VMEM((experts, width, 2 * hid), BF16)
    down_buf = pltpu.VMEM((experts, hid, width), BF16)
    part_shapes = (sds((2, half, width), BF16),) * 16

    pre, hidden = pl.pallas_call(
        forward_kernel,
        out_shape=(sds((experts, quad_rows, 2 * hid), F32), sds((experts, quad_rows, hid), BF16)),
        in_specs=[SMEM, VMEM, VMEM] + [ANY] * 20,
        out_specs=(VMEM, VMEM),
        scratch_shapes=[token_buf, row_buf, up_buf, DMA((16,)), DMA((10,))],
        compiler_params=PARAMS,
        cost_estimate=cost(7 * 10**9, 26 << 20),
    )(pos, pick, rowgate, *gathered(tokens), *ups)

    parts = pl.pallas_call(
        output_kernel,
        out_shape=part_shapes,
        in_specs=[SMEM, VMEM, VMEM] + [ANY] * 10,
        out_specs=(ANY,) * 16,
        scratch_shapes=[token_buf, row_buf, down_buf, DMA((10,)), DMA((16,))],
        compiler_params=PARAMS,
        cost_estimate=cost(5 * 10**9, 16 << 20),
    )(pos, hidden, pickt, *downs)
    mixed = scattered(parts)

    grad_parts = pl.pallas_call(
        backward_kernel,
        out_shape=part_shapes,
        in_specs=[SMEM] + [VMEM] * 4 + [ANY] * 30,
        out_specs=(ANY,) * 16,
        scratch_shapes=[
            token_buf,
            row_buf,
            row_buf,
            up_buf,
            down_buf,
            pltpu.VMEM((quad_rows, 2 * hid), BF16),
            DMA((16,)),
            DMA((10,)),
            DMA((10,)),
            DMA((16,)),
        ],
        compiler_params=PARAMS,
        cost_estimate=cost(12 * 10**9, 40 << 20),
    )(pos, pick, pickt, rowgate, pre, *gathered(cotangent), *ups, *downs)
    tokens_grad = scattered(grad_parts)
    return (mixed, tokens_grad)


def solution(mesh):
    rows = P(("dp", "expert"), None)
    placed = (rows, rows, rows, rows, rows, P("expert", "dp", None), P("expert", None, "dp"))
    return jax.shard_map(
        body, mesh=mesh, in_specs=placed, out_specs=(rows, rows), check_vma=False
    )
```

```python
import jax
import jax.numpy as jnp
from jax import lax
from jax.experimental import pallas as pl
from jax.experimental.pallas import tpu as pltpu
from jax.sharding import PartitionSpec as P


F32 = jnp.float32
BF16 = jnp.bfloat16
ANY = pl.BlockSpec(memory_space=pl.ANY)
VMEM = pl.BlockSpec(memory_space=pltpu.VMEM)
SMEM = pl.BlockSpec(memory_space=pltpu.SMEM)
QUADS = ((0, 0), (0, 1), (1, 0), (1, 1))
TILE = 512


def hop(value, along, step):
    side = 4
    pairs = []
    for x in range(side):
        for y in range(side):
            to = ((x + step) % side, y) if along == "x" else (x, (y + step) % side)
            pairs.append((x * side + y, to[0] * side + to[1]))
    return lax.ppermute(value, "expert", pairs)


def shift(value, step):
    count = lax.axis_size("dp")
    return lax.ppermute(value, "dp", [(i, (i + 2 * step) % count) for i in range(count)])


def swap(value):
    return lax.ppermute(value, "dp", [(i, i ^ 1) for i in range(lax.axis_size("dp"))])


def ring_gather(own, along):
    half = own.shape[0] // 2
    before = hop(own, along, 1)
    after = hop(own, along, -1)
    far_low = hop(before[:half], along, 1)
    far_high = hop(after[half:], along, -1)
    return before, after, far_low, far_high


def torus_gather(rows, first, second):
    line = ring_gather(rows, first)
    again, *_ = lax.optimization_barrier((rows, line[0], line[1]))
    own = ring_gather(again, second)
    rest = jnp.concatenate(line, axis=0)
    return (rows, rest) + own + ring_gather(rest, second)


def z_gather(piece):
    half = piece.shape[0] // 2
    before = shift(piece, 1)
    after = shift(piece, -1)
    far = [shift(before[:half], 1), shift(after[half:], -1)]
    pieces = [piece, before, after] + far
    return pieces + [swap(p) for p in pieces]


def add(*terms):
    return sum(t.astype(F32) for t in terms).astype(BF16)


def ring_scatter(own, back, ahead, far, along):
    from_back = hop(far[0], along, 1)
    from_ahead = hop(far[1], along, -1)
    plain_up = hop(ahead[1], along, 1)
    plain_down = hop(back[0], along, -1)
    up = hop(add(ahead[0], from_back), along, 1)
    down = hop(add(back[1], from_ahead), along, -1)
    return add(own[0], up, plain_down), add(own[1], plain_up, down)


def torus_scatter(parts, first, second):
    pairs = [(parts[2 * i], parts[2 * i + 1]) for i in range(4)]
    low, high = ring_scatter(*pairs, first)
    half = low.shape[1] // 2
    cut = [(v[i, :half], v[i, half:]) for v in (low, high) for i in (0, 1)]
    return jnp.concatenate(ring_scatter(*cut, second), axis=0)


def small_gather(value):
    for along in ("x", "y"):
        value = jnp.concatenate([value, hop(value, along, 1)], axis=0)
        value = jnp.concatenate([value, hop(value, along, 2)], axis=0)
    return value


def block_pieces(refs, outer, inner):
    count = refs[0].shape[0]
    half = count // 2
    start = (inner - 1) * count
    if outer < 3:
        if inner == 0:
            return [((refs[0], refs[2], refs[3])[outer], 0, count)]
        ref = (refs[1], refs[6], refs[7])[outer]
        return [(ref.at[pl.ds(start, count)], 0, count)]
    if inner == 0:
        return [(refs[4], 0, half), (refs[5], half, half)]
    if inner == 1:
        return [(refs[8].at[pl.ds(0, count)], 0, count)]
    if inner == 3:
        return [(refs[9].at[pl.ds(half, count)], 0, count)]
    return [(refs[8].at[pl.ds(count, half)], 0, half), (refs[9].at[pl.ds(0, half)], half, half)]


def block_copies(refs, quad, slot, buf, sems, turned):
    out = []
    for n, y, x in quad_owners(quad):
        for i, (ref, at, rows) in enumerate(block_pieces(refs, *((x, y) if turned else (y, x)))):
            dst = buf.at[slot, n, pl.ds(at, rows)]
            out.append(pltpu.make_async_copy(ref, dst, sems.at[slot, n, i]))
    return out


def quad_owners(q):
    qy, qx = QUADS[q]
    return [(2 * y + x, 2 * qy + y, 2 * qx + x) for y in range(2) for x in range(2)]


def weight_copies(pos_ref, refs, buf, sems):
    me = pos_ref[0]
    core = lax.rem(me, 2)
    width = refs[0].shape[1]
    out = [[] for _ in range(buf.shape[0])]
    for n, ref in enumerate(refs):
        k = n % 5
        chip = lax.rem(lax.div(me, 2) + (0, 3, 1, 2, 2)[k], 4)
        at = 2 * chip + (core if n < 5 else 1 - core)
        count = ref.shape[0]
        for i in range(count):
            j = i + (count if k == 4 else 0)
            dst = buf.at[j, pl.ds(pl.multiple_of(at * width, width), width)]
            sem = sems.at[j, min(k, 3) + (4 if n >= 5 else 0)]
            out[j].append(pltpu.make_async_copy(ref.at[i], dst, sem))
    return out


def pick_kernel(row_ref, rowt_ref, gate_ref, pick_ref, pickt_ref, rowgate_ref):
    rows, tokens = pick_ref.shape[1:]
    per = rows // 4
    top = row_ref.shape[1]
    for p in range(pick_ref.shape[0]):
        down = lax.broadcasted_iota(jnp.int32, (rows, tokens), 0)
        hits = jnp.zeros((rows, tokens), F32)
        gates = jnp.zeros((rows, tokens), F32)
        for k in range(top):
            same = down == row_ref[p, k : k + 1, :]
            hits = jnp.where(same, 1.0, hits)
            gates = jnp.where(same, gate_ref[p, k : k + 1, :], gates)
        pick_ref[p] = hits.astype(BF16)
        sums = jnp.sum(gates, axis=1, keepdims=True)
        at = p % 2 * per
        for j in range(4):
            rowgate_ref[p // 2, j, at : at + per] = jnp.broadcast_to(
                sums[j * per : (j + 1) * per], (per, 128)
            )
        across = lax.broadcasted_iota(jnp.int32, (tokens, rows), 1)
        hits = jnp.zeros((tokens, rows), F32)
        for k in range(top):
            hits = jnp.where(across == rowt_ref[p, :, k : k + 1], 1.0, hits)
        pickt_ref[p] = hits.astype(BF16)


def columns(width, step):
    def run(c, carry):
        step(pl.ds(pl.multiple_of(c * TILE, TILE), TILE))
        return carry

    lax.fori_loop(0, width // TILE, run, 0)


def combine_quad(q, pickt_ref, rows_buf, buf):
    per = rows_buf.shape[1] // 2

    def combine(at):
        for i in range(2):
            rows = rows_buf[:, i * per : (i + 1) * per, at].reshape(-1, TILE)
            sums = jnp.dot(pickt_ref[2 * q + i], rows, preferred_element_type=F32)
            buf[2 * i : 2 * i + 2, :, at] = sums.astype(BF16).reshape(2, -1, TILE)

    columns(buf.shape[-1], combine)


def part_copies(q, buf, refs, turned, sems):
    out = []
    for n, y, x in quad_owners(q):
        outer, inner = (x, y) if turned else (y, x)
        ref = refs[2 * (outer % 2) + inner // 2].at[inner % 2]
        out.append(pltpu.make_async_copy(buf.at[n], ref, sems.at[n]))
    return out


def experts_kernel(pos_ref, pick_ref, pickt_ref, rowgate_ref, *refs):
    token_refs, cot_refs, weight_refs = refs[:10], refs[10:20], refs[20:30]
    mixed_refs, grad_refs, kept_rows_ref, kept_grads_ref = refs[30:34], refs[34:38], refs[38], refs[39]
    tokens, cots, token_rows, cot_rows, weight, grad = refs[40:46]
    token_sems, cot_sems, weight_sems, out_sems, kept_sems = refs[46:]
    width = weight.shape[1]
    hid = weight.shape[2] // 3
    per = token_rows.shape[2] // 2
    nt = (((1,), (1,)), ((), ()))
    loads = []
    for q in range(4):
        copies = block_copies(token_refs, q, q, tokens, token_sems, False)
        loads.append((q, tokens, token_rows, copies))
    for q in range(4):
        copies = block_copies(cot_refs, q, q, cots, cot_sems, True)
        loads.append((q, cots, cot_rows, copies))
    queue = [load[-1] for load in loads] + weight_copies(pos_ref, weight_refs, weight, weight_sems)
    ahead = 3
    for copies in queue[:ahead]:
        for c in copies:
            c.start()
    for n, (q, buf, rows_buf, copies) in enumerate(loads):
        for c in copies:
            c.wait()
        more = queue[n + ahead : n + ahead + 1] if n < 7 else queue[n + ahead :]
        for later in more:
            for c in later:
                c.start()

        def gather(at, q=q, buf=buf, rows_buf=rows_buf):
            for i in range(2):
                values = buf[q, 2 * i : 2 * i + 2, :, at].reshape(-1, TILE)
                rows = jnp.dot(pick_ref[2 * q + i], values, preferred_element_type=F32)
                rows_buf[q, :, i * per : (i + 1) * per, at] = rows.astype(BF16).reshape(4, per, TILE)

        columns(width, gather)

    def expert(j, carry):
        for n in range(weight_sems.shape[1]):
            some = weight_refs[3].at[0]
            pltpu.make_async_copy(
                some, weight.at[j, pl.ds(0, some.shape[0])], weight_sems.at[j, n]
            ).wait()
        rows = grad.shape[0]
        pre = jnp.dot(
            token_rows[:, j].reshape(rows, width),
            weight[j, :, : 2 * hid],
            preferred_element_type=F32,
        )
        back = jnp.dot(
            cot_rows[:, j].reshape(rows, width),
            weight[j, :, 2 * hid :],
            preferred_element_type=F32,
        )
        gate = rowgate_ref[:, j].reshape(rows, 128)[:, :1]
        g, u = pre[:, :hid], pre[:, hid:]
        s = 1.0 / (1.0 + jnp.exp(-g))
        back = back * gate
        grad[:, :hid] = (back * u * s * (1.0 + g * (1.0 - s))).astype(BF16)
        grad[:, hid : 2 * hid] = (back * (g * s)).astype(BF16)
        grad[:, 2 * hid :] = (gate * (g * s) * u).astype(BF16)

        def outs(at):
            out = lax.dot_general(
                grad[:, 2 * hid :], weight[j, at, 2 * hid :], nt, preferred_element_type=F32
            )
            token_rows[:, j, :, at] = out.astype(BF16).reshape(4, -1, TILE)
            out = lax.dot_general(
                grad[:, : 2 * hid], weight[j, at, : 2 * hid], nt, preferred_element_type=F32
            )
            cot_rows[:, j, :, at] = out.astype(BF16).reshape(4, -1, TILE)

        columns(width, outs)
        return carry

    lax.fori_loop(0, 4, expert, 0)
    copies = []
    for side, (buf, rows_buf, refs) in enumerate(
        ((tokens, token_rows, mixed_refs), (cots, cot_rows, grad_refs))
    ):
        for q in GIVE_FIRST[side]:
            combine_quad(q, pickt_ref, rows_buf.at[q], buf.at[q])
            some = part_copies(q, buf.at[q], refs, bool(side), out_sems.at[side, q])
            for c in some:
                c.start()
            copies += some
    for side, (rows_buf, kept_ref) in enumerate(
        ((token_rows, kept_rows_ref), (cot_rows, kept_grads_ref))
    ):
        for n, q in enumerate(GIVE_LATER[side]):
            c = pltpu.make_async_copy(rows_buf.at[q], kept_ref.at[n], kept_sems.at[side, n])
            c.start()
            copies.append(c)
    for c in copies:
        c.wait()


def later_kernel(pickt_ref, kept_rows_ref, kept_grads_ref, *refs):
    mixed_refs, grad_refs, rows_buf, buf, in_sems, out_sems = refs[:4], refs[4:8], *refs[8:]
    loads = []
    for side, kept_ref in enumerate((kept_rows_ref, kept_grads_ref)):
        for n in range(2):
            c = pltpu.make_async_copy(kept_ref.at[n], rows_buf.at[side, n], in_sems.at[side, n])
            c.start()
            loads.append(c)
    copies = []
    for side, refs in enumerate((mixed_refs, grad_refs)):
        for n, q in enumerate(GIVE_LATER[side]):
            loads[2 * side + n].wait()
            combine_quad(q, pickt_ref, rows_buf.at[side, n], buf.at[side, n])
            some = part_copies(q, buf.at[side, n], refs, bool(side), out_sems.at[side, n])
            for c in some:
                c.start()
            copies += some
    for c in copies:
        c.wait()


def cost(flops, moved):
    return pl.CostEstimate(flops=flops, bytes_accessed=moved, transcendentals=0)


GIVE_FIRST = ((2, 3), (1, 3))
GIVE_LATER = ((0, 1), (0, 2))
PARAMS = pltpu.CompilerParams(vmem_limit_bytes=60 * 1024 * 1024)
DMA = pltpu.SemaphoreType.DMA


def body(tokens, cotangent, expert_ids, slot_ids, gate_weights, w_gate_up, w_down):
    tok_count, width = tokens.shape
    top = expert_ids.shape[1]
    experts = w_gate_up.shape[0]
    hid = w_down.shape[1]
    group = lax.axis_size("expert")
    capacity = 5 * tok_count * top // (4 * experts * group)
    local_rows = experts * capacity
    pair_tokens = 2 * tok_count
    pair_rows = 2 * local_rows
    sds = jax.ShapeDtypeStruct

    places = (expert_ids * capacity + slot_ids).astype(F32).T
    info = small_gather(jnp.concatenate([places, gate_weights.T], axis=0)[None])
    info = info.reshape(4, 4, 2 * top, tok_count)
    info = jnp.stack([info[0], info[1], info[3], info[2]])
    info = jnp.stack([info[:, 0], info[:, 1], info[:, 3], info[:, 2]], axis=1)
    info = info.reshape(2, 2, 2, 2, 2 * top, tok_count)
    owner = jnp.arange(2)[None, None, None, :, None, None]
    place = info[:, :, :, :, :top].astype(jnp.int32) - lax.axis_index("expert") * local_rows
    mine = (place >= 0) & (place < local_rows)
    row = place // capacity * (2 * capacity) + owner * capacity + place % capacity
    row = jnp.where(mine, row, -1)
    by_pair = lambda v: v.transpose(0, 2, 1, 4, 3, 5).reshape(8, top, pair_tokens)
    row = by_pair(row)
    gates = by_pair(info[:, :, :, :, top:])
    picks = pl.pallas_call(
        pick_kernel,
        out_shape=(
            sds((8, pair_rows, pair_tokens), BF16),
            sds((8, pair_tokens, pair_rows), BF16),
            sds((4, experts, 4 * capacity, 128), F32),
        ),
        in_specs=[VMEM] * 3,
        out_specs=(VMEM,) * 3,
        compiler_params=PARAMS,
        cost_estimate=cost(0, 8 << 20),
    )
    pick, pickt, rowgate = picks(row, jnp.swapaxes(row, 1, 2), gates)

    pos = lax.axis_index("dp").astype(jnp.int32).reshape(1)
    weights = z_gather(jnp.concatenate([w_gate_up, jnp.swapaxes(w_down, 1, 2)], axis=2))
    part = sds((2, tok_count, width), BF16)
    kept = sds((2, experts, 4 * capacity, width), BF16)
    token_buf = pltpu.VMEM((4, 4, tok_count, width), BF16)
    row_buf = pltpu.VMEM((4, experts, 4 * capacity, width), BF16)
    through = pl.pallas_call(
        experts_kernel,
        out_shape=(part,) * 8 + (kept, kept),
        in_specs=[SMEM] + [VMEM] * 3 + [ANY] * 30,
        out_specs=(ANY,) * 10,
        scratch_shapes=[
            token_buf,
            token_buf,
            row_buf,
            row_buf,
            pltpu.VMEM((experts, width, 3 * hid), BF16),
            pltpu.VMEM((16 * capacity, 3 * hid), BF16),
            DMA((4, 4, 2)),
            DMA((4, 4, 2)),
            DMA((experts, 8)),
            DMA((2, 4, 4)),
            DMA((2, 2)),
        ],
        compiler_params=PARAMS,
        cost_estimate=cost(20 * 10**9, 60 << 20),
    )
    done = through(
        pos,
        pick,
        pickt,
        rowgate,
        *torus_gather(tokens, "x", "y"),
        *torus_gather(cotangent, "y", "x"),
        *weights,
    )
    later = pl.pallas_call(
        later_kernel,
        out_shape=(part,) * 8,
        in_specs=[VMEM, ANY, ANY],
        out_specs=(ANY,) * 8,
        scratch_shapes=[
            pltpu.VMEM((2, 2, experts, 4 * capacity, width), BF16),
            pltpu.VMEM((2, 2, 4, tok_count, width), BF16),
            DMA((2, 2)),
            DMA((2, 2, 4)),
        ],
        compiler_params=PARAMS,
        cost_estimate=cost(3 * 10**9, 15 << 20),
    )
    rest = later(pickt, done[8], done[9])
    mixed = torus_scatter(rest[:4] + done[:4], "y", "x")
    grads = torus_scatter(rest[4:] + done[4:8], "x", "y")
    return (mixed, grads)


def solution(mesh):
    rows = P(("dp", "expert"), None)
    placed = (rows, rows, rows, rows, rows, P("expert", "dp", None), P("expert", None, "dp"))

    return jax.shard_map(body, mesh=mesh, in_specs=placed, out_specs=(rows, rows), check_vma=False)
```

```python
import jax
import jax.numpy as jnp
from jax import lax
from jax.experimental import pallas as pl
from jax.experimental.pallas import tpu as pltpu
from jax.sharding import PartitionSpec as P


F32 = jnp.float32
BF16 = jnp.bfloat16
ANY = pl.BlockSpec(memory_space=pl.ANY)
VMEM = pl.BlockSpec(memory_space=pltpu.VMEM)
SMEM = pl.BlockSpec(memory_space=pltpu.SMEM)
QUADS = ((0, 0), (0, 1), (1, 0), (1, 1))
TILE = 512


def hop(value, along, step):
    side = 4
    pairs = []
    for x in range(side):
        for y in range(side):
            to = ((x + step) % side, y) if along == "x" else (x, (y + step) % side)
            pairs.append((x * side + y, to[0] * side + to[1]))
    return lax.ppermute(value, "expert", pairs)


def shift(value, step):
    count = lax.axis_size("dp")
    return lax.ppermute(value, "dp", [(i, (i + 2 * step) % count) for i in range(count)])


def swap(value):
    return lax.ppermute(value, "dp", [(i, i ^ 1) for i in range(lax.axis_size("dp"))])


def ring_gather(own, along):
    half = own.shape[0] // 2
    before = hop(own, along, 1)
    after = hop(own, along, -1)
    far_low = hop(before[:half], along, 1)
    far_high = hop(after[half:], along, -1)
    return before, after, far_low, far_high


def torus_gather(rows, first, second):
    line = ring_gather(rows, first)
    own = ring_gather(rows, second)
    rest = jnp.concatenate(line, axis=0)
    return (rows, rest) + own + ring_gather(rest, second)


def z_gather(piece):
    half = piece.shape[0] // 2
    before = shift(piece, 1)
    after = shift(piece, -1)
    low, high = before[:half], after[half:]
    far = [shift(low, 1), shift(high, -1)]
    pieces = [piece, before, after] + far
    return pieces + [swap(p) for p in pieces]


def add(*terms):
    return sum(t.astype(F32) for t in terms).astype(BF16)


def ring_scatter(own, back, ahead, far, along):
    from_back = hop(far[0], along, 1)
    from_ahead = hop(far[1], along, -1)
    plain_up = hop(ahead[1], along, 1)
    plain_down = hop(back[0], along, -1)
    up = hop(add(ahead[0], from_back), along, 1)
    down = hop(add(back[1], from_ahead), along, -1)
    return add(own[0], up, plain_down), add(own[1], plain_up, down)


def torus_scatter(parts, first, second):
    own, back, ahead, far = [(parts[2 * i], parts[2 * i + 1]) for i in range(4)]
    from_back = hop(far[0], first, 1)
    from_ahead = hop(far[1], first, -1)
    plain_up = hop(ahead[1], first, 1)
    plain_down = hop(back[0], first, -1)
    down = [None, None]
    up = [None, None]
    for i in (1, 0):
        down[i] = hop(add(back[1][i], from_ahead[i]), first, -1)
        up[i] = hop(add(ahead[0][i], from_back[i]), first, 1)
    sums = [add(own[0][i], up[i], plain_down[i]) for i in (0, 1)]
    sums += [add(own[1][i], plain_up[i], down[i]) for i in (0, 1)]
    half = sums[0].shape[0] // 2
    cut = [(v[:half], v[half:]) for v in sums]
    return jnp.concatenate(ring_scatter(*cut, second), axis=0)


def small_gather(value):
    for along in ("x", "y"):
        value = jnp.concatenate([value, hop(value, along, 1)], axis=0)
        value = jnp.concatenate([value, hop(value, along, 2)], axis=0)
    return value


def block_pieces(refs, outer, inner):
    count = refs[0].shape[0]
    half = count // 2
    start = (inner - 1) * count
    if outer < 3:
        if inner == 0:
            return [((refs[0], refs[2], refs[3])[outer], 0, count)]
        ref = (refs[1], refs[6], refs[7])[outer]
        return [(ref.at[pl.ds(start, count)], 0, count)]
    if inner == 0:
        return [(refs[4], 0, half), (refs[5], half, half)]
    if inner == 1:
        return [(refs[8].at[pl.ds(0, count)], 0, count)]
    if inner == 3:
        return [(refs[9].at[pl.ds(half, count)], 0, count)]
    return [(refs[8].at[pl.ds(count, half)], 0, half), (refs[9].at[pl.ds(0, half)], half, half)]


def block_copies(refs, quad, slot, buf, sems, turned):
    out = []
    for n, y, x in quad_owners(quad):
        for ref, at, rows in block_pieces(refs, *((x, y) if turned else (y, x))):
            dst = buf.at[slot, n, pl.ds(at, rows)]
            out.append(pltpu.make_async_copy(ref, dst, sems.at[slot]))
    return out


def quad_owners(q):
    qy, qx = QUADS[q]
    return [(2 * y + x, 2 * qy + y, 2 * qx + x) for y in range(2) for x in range(2)]


def weight_copies(pos_ref, refs, buf, sems):
    me = pos_ref[0]
    core = lax.rem(me, 2)
    width = refs[0].shape[1]
    out = [[] for _ in range(buf.shape[0])]
    for n, ref in enumerate(refs):
        k = n % 5
        chip = lax.rem(lax.div(me, 2) + (0, 3, 1, 2, 2)[k], 4)
        at = 2 * chip + (core if n < 5 else 1 - core)
        count = ref.shape[0]
        for i in range(count):
            j = i + (count if k == 4 else 0)
            dst = buf.at[j, pl.ds(pl.multiple_of(at * width, width), width)]
            out[j].append(pltpu.make_async_copy(ref.at[i], dst, sems.at[j]))
    return out


def pick_kernel(row_ref, rowt_ref, gate_ref, pick_ref, pickt_ref, rowgate_ref):
    rows, tokens = pick_ref.shape[1:]
    per = rows // 4
    top = row_ref.shape[1]

    def pair(p, carry):
        at = pl.ds(pl.multiple_of(lax.rem(p, 2) * per, 8), per)
        down = lax.broadcasted_iota(jnp.int32, (rows, tokens), 0)
        hits = jnp.zeros((rows, tokens), F32)
        gates = jnp.zeros((rows, tokens), F32)
        for k in range(top):
            same = down == row_ref[p, k : k + 1, :]
            hits = jnp.where(same, 1.0, hits)
            gates = jnp.where(same, gate_ref[p, k : k + 1, :], gates)
        pick_ref[p] = hits.astype(BF16)
        sums = jnp.sum(gates, axis=1, keepdims=True)
        for j in range(4):
            rowgate_ref[lax.div(p, 2), j, at] = jnp.broadcast_to(
                sums[j * per : (j + 1) * per], (per, 128)
            )
        across = lax.broadcasted_iota(jnp.int32, (tokens, rows), 1)
        hits = jnp.zeros((tokens, rows), F32)
        for k in range(top):
            hits = jnp.where(across == rowt_ref[p, :, k : k + 1], 1.0, hits)
        pickt_ref[p] = hits.astype(BF16)
        return carry

    lax.fori_loop(0, pick_ref.shape[0], pair, 0)


def columns(width, step):
    def run(c, carry):
        step(pl.ds(pl.multiple_of(c * TILE, TILE), TILE))
        return carry

    lax.fori_loop(0, width // TILE, run, 0)


def combine_quad(q, pickt_ref, rows_buf, buf):
    per = rows_buf.shape[1] // 2

    def combine(at):
        for i in range(2):
            rows = rows_buf[:, i * per : (i + 1) * per, at].reshape(-1, TILE)
            sums = jnp.dot(pickt_ref[2 * q + i], rows, preferred_element_type=F32)
            buf[2 * i : 2 * i + 2, :, at] = sums.astype(BF16).reshape(2, -1, TILE)

    columns(buf.shape[-1], combine)


def part_copies(q, buf, refs, turned, sems):
    out = []
    for n, y, x in quad_owners(q):
        outer, inner = (x, y) if turned else (y, x)
        ref = refs[2 * (outer % 2) + inner // 2].at[inner % 2]
        out.append(pltpu.make_async_copy(buf.at[n], ref, sems.at[n]))
    return out


def experts_kernel(pos_ref, pick_ref, pickt_ref, rowgate_ref, *refs):
    token_refs, cot_refs, weight_refs = refs[:10], refs[10:20], refs[20:30]
    mixed_refs, grad_refs, kept_rows_ref, kept_grads_ref = refs[30:34], refs[34:38], refs[38], refs[39]
    tokens, cots, token_rows, cot_rows, weight, grad = refs[40:46]
    token_sems, cot_sems, weight_sems, out_sems, kept_sems = refs[46:]
    width = weight.shape[1]
    hid = weight.shape[2] // 3
    per = token_rows.shape[2] // 2
    nt = (((1,), (1,)), ((), ()))
    weights = weight_copies(pos_ref, weight_refs, weight, weight_sems)
    for q in range(4):
        for c in block_copies(token_refs, q, q, tokens, token_sems, False):
            c.start()
    for q in range(4):
        for c in block_copies(cot_refs, q, q, cots, cot_sems, True):
            c.start()

    def gather_all(buf, rows_buf, sems):
        def gather_quad(q, carry):
            pltpu.make_async_copy(buf.at[q], buf.at[q], sems.at[q]).wait()

            def gather(at):
                for i in range(2):
                    values = buf[q, 2 * i : 2 * i + 2, :, at].reshape(-1, TILE)
                    rows = jnp.dot(pick_ref[2 * q + i], values, preferred_element_type=F32)
                    rows = rows.astype(BF16).reshape(4, per, TILE)
                    rows_buf[q, :, i * per : (i + 1) * per, at] = rows

            columns(width, gather)
            return carry

        lax.fori_loop(0, 4, gather_quad, 0)

    for c in weights[0]:
        c.start()
    gather_all(tokens, token_rows, token_sems)
    for copies in weights[1:]:
        for c in copies:
            c.start()
    gather_all(cots, cot_rows, cot_sems)

    def expert(j, carry):
        pltpu.make_async_copy(weight.at[j], weight.at[j], weight_sems.at[j]).wait()
        rows = grad.shape[0]
        pre = jnp.dot(
            token_rows[:, j].reshape(rows, width),
            weight[j, :, : 2 * hid],
            preferred_element_type=F32,
        )
        back = jnp.dot(
            cot_rows[:, j].reshape(rows, width),
            weight[j, :, 2 * hid :],
            preferred_element_type=F32,
        )
        gate = rowgate_ref[:, j].reshape(rows, 128)[:, :1]
        g, u = pre[:, :hid], pre[:, hid:]
        s = 1.0 / (1.0 + jnp.exp(-g))
        back = back * gate
        grad[:, :hid] = (back * u * s * (1.0 + g * (1.0 - s))).astype(BF16)
        grad[:, hid : 2 * hid] = (back * (g * s)).astype(BF16)
        grad[:, 2 * hid :] = (gate * (g * s) * u).astype(BF16)

        def outs(at):
            out = lax.dot_general(
                grad[:, 2 * hid :], weight[j, at, 2 * hid :], nt, preferred_element_type=F32
            )
            token_rows[:, j, :, at] = out.astype(BF16).reshape(4, -1, TILE)
            out = lax.dot_general(
                grad[:, : 2 * hid], weight[j, at, : 2 * hid], nt, preferred_element_type=F32
            )
            cot_rows[:, j, :, at] = out.astype(BF16).reshape(4, -1, TILE)

        columns(width, outs)
        return carry

    lax.fori_loop(0, 4, expert, 0)
    copies = []
    for side, (buf, rows_buf, refs) in enumerate(
        ((tokens, token_rows, mixed_refs), (cots, cot_rows, grad_refs))
    ):


        def combine(n, carry, side=side, buf=buf, rows_buf=rows_buf):
            q = 1 + 2 * n if side else 2 + n
            combine_quad(q, pickt_ref, rows_buf.at[q], buf.at[q])
            return carry

        lax.fori_loop(0, 2, combine, 0)
        for q in GIVE_FIRST[side]:
            some = part_copies(q, buf.at[q], refs, bool(side), out_sems.at[side, q])
            for c in some:
                c.start()
            copies += some
    for side, (rows_buf, kept_ref) in enumerate(
        ((token_rows, kept_rows_ref), (cot_rows, kept_grads_ref))
    ):
        for n, q in enumerate(GIVE_LATER[side]):
            c = pltpu.make_async_copy(rows_buf.at[q], kept_ref.at[n], kept_sems.at[side, n])
            c.start()
            copies.append(c)
    for c in copies:
        c.wait()


def later_kernel(pickt_ref, kept_rows_ref, kept_grads_ref, *refs):
    mixed_refs, grad_refs, rows_buf, buf, in_sems, out_sems = refs[:4], refs[4:8], *refs[8:]
    loads = []
    for side, kept_ref in enumerate((kept_rows_ref, kept_grads_ref)):
        for n in range(2):
            c = pltpu.make_async_copy(kept_ref.at[n], rows_buf.at[side, n], in_sems.at[side, n])
            c.start()
            loads.append(c)
    for c in loads:
        c.wait()

    def combine(m, carry):
        side, n = lax.div(m, 2), lax.rem(m, 2)
        combine_quad(n * (1 + side), pickt_ref, rows_buf.at[side, n], buf.at[side, n])
        return carry

    lax.fori_loop(0, 4, combine, 0)
    copies = []
    for side, refs in enumerate((mixed_refs, grad_refs)):
        for n, q in enumerate(GIVE_LATER[side]):
            copies += part_copies(q, buf.at[side, n], refs, bool(side), out_sems.at[side, n])
    for c in copies:
        c.start()
    for c in copies:
        c.wait()


def cost(flops, moved):
    return pl.CostEstimate(flops=flops, bytes_accessed=moved, transcendentals=0)


GIVE_FIRST = ((2, 3), (1, 3))
GIVE_LATER = ((0, 1), (0, 2))
PARAMS = pltpu.CompilerParams(vmem_limit_bytes=60 * 1024 * 1024)
DMA = pltpu.SemaphoreType.DMA


def body(tokens, cotangent, expert_ids, slot_ids, gate_weights, w_gate_up, w_down):
    tok_count, width = tokens.shape
    top = expert_ids.shape[1]
    experts = w_gate_up.shape[0]
    hid = w_down.shape[1]
    group = lax.axis_size("expert")
    capacity = 5 * tok_count * top // (4 * experts * group)
    local_rows = experts * capacity
    pair_tokens = 2 * tok_count
    pair_rows = 2 * local_rows
    sds = jax.ShapeDtypeStruct

    places = (expert_ids * capacity + slot_ids).astype(F32).T
    info = small_gather(jnp.concatenate([places, gate_weights.T], axis=0)[None])
    info = info.reshape(4, 4, 2 * top, tok_count)
    info = jnp.stack([info[0], info[1], info[3], info[2]])
    info = jnp.stack([info[:, 0], info[:, 1], info[:, 3], info[:, 2]], axis=1)
    info = info.reshape(2, 2, 2, 2, 2 * top, tok_count)
    owner = jnp.arange(2)[None, None, None, :, None, None]
    place = info[:, :, :, :, :top].astype(jnp.int32) - lax.axis_index("expert") * local_rows
    mine = (place >= 0) & (place < local_rows)
    row = place // capacity * (2 * capacity) + owner * capacity + place % capacity
    row = jnp.where(mine, row, -1)
    by_pair = lambda v: v.transpose(0, 2, 1, 4, 3, 5).reshape(8, top, pair_tokens)
    row = by_pair(row)
    gates = by_pair(info[:, :, :, :, top:])
    picks = pl.pallas_call(
        pick_kernel,
        out_shape=(
            sds((8, pair_rows, pair_tokens), BF16),
            sds((8, pair_tokens, pair_rows), BF16),
            sds((4, experts, 4 * capacity, 128), F32),
        ),
        in_specs=[VMEM] * 3,
        out_specs=(VMEM,) * 3,
        compiler_params=PARAMS,
        cost_estimate=cost(0, 8 << 20),
    )
    pick, pickt, rowgate = picks(row, jnp.swapaxes(row, 1, 2), gates)

    pos = lax.axis_index("dp").astype(jnp.int32).reshape(1)
    weights = z_gather(jnp.concatenate([w_gate_up, jnp.swapaxes(w_down, 1, 2)], axis=2))
    part = sds((2, tok_count, width), BF16)
    kept = sds((2, experts, 4 * capacity, width), BF16)
    token_buf = pltpu.VMEM((4, 4, tok_count, width), BF16)
    row_buf = pltpu.VMEM((4, experts, 4 * capacity, width), BF16)
    through = pl.pallas_call(
        experts_kernel,
        out_shape=(part,) * 8 + (kept, kept),
        in_specs=[SMEM] + [VMEM] * 3 + [ANY] * 30,
        out_specs=(ANY,) * 10,
        scratch_shapes=[
            token_buf,
            token_buf,
            row_buf,
            row_buf,
            pltpu.VMEM((experts, width, 3 * hid), BF16),
            pltpu.VMEM((16 * capacity, 3 * hid), BF16),
            DMA((4,)),
            DMA((4,)),
            DMA((experts,)),
            DMA((2, 4, 4)),
            DMA((2, 2)),
        ],
        compiler_params=PARAMS,
        cost_estimate=cost(20 * 10**9, 60 << 20),
    )
    done = through(
        pos,
        pick,
        pickt,
        rowgate,
        *torus_gather(tokens, "x", "y"),
        *torus_gather(cotangent, "y", "x"),
        *weights,
    )
    later = pl.pallas_call(
        later_kernel,
        out_shape=(part,) * 8,
        in_specs=[VMEM, ANY, ANY],
        out_specs=(ANY,) * 8,
        scratch_shapes=[
            pltpu.VMEM((2, 2, experts, 4 * capacity, width), BF16),
            pltpu.VMEM((2, 2, 4, tok_count, width), BF16),
            DMA((2, 2)),
            DMA((2, 2, 4)),
        ],
        compiler_params=PARAMS,
        cost_estimate=cost(3 * 10**9, 15 << 20),
    )
    rest = later(pickt, done[8], done[9])
    mixed = torus_scatter(rest[:4] + done[:4], "y", "x")
    grads = torus_scatter(rest[4:] + done[4:8], "x", "y")
    return (mixed, grads)


def solution(mesh):
    rows = P(("dp", "expert"), None)
    placed = (rows, rows, rows, rows, rows, P("expert", "dp", None), P("expert", None, "dp"))

    return jax.shard_map(body, mesh=mesh, in_specs=placed, out_specs=(rows, rows), check_vma=False)
```

```python
import jax
import jax.numpy as jnp
from jax import lax
from jax.experimental import pallas as pl
from jax.experimental.pallas import tpu as pltpu
from jax.sharding import PartitionSpec as P


F32 = jnp.float32
BF16 = jnp.bfloat16
ANY = pl.BlockSpec(memory_space=pl.ANY)
VMEM = pl.BlockSpec(memory_space=pltpu.VMEM)
SMEM = pl.BlockSpec(memory_space=pltpu.SMEM)
QUADS = ((0, 0), (0, 1), (1, 0), (1, 1))
TILE = 512


def hop(value, along, step):
    side = 4
    pairs = []
    for x in range(side):
        for y in range(side):
            to = ((x + step) % side, y) if along == "x" else (x, (y + step) % side)
            pairs.append((x * side + y, to[0] * side + to[1]))
    return lax.ppermute(value, "expert", pairs)


def shift(value, step):
    count = lax.axis_size("dp")
    return lax.ppermute(value, "dp", [(i, (i + 2 * step) % count) for i in range(count)])


def swap(value):
    return lax.ppermute(value, "dp", [(i, i ^ 1) for i in range(lax.axis_size("dp"))])


def ring_gather(own, along):
    half = own.shape[0] // 2
    before = hop(own, along, 1)
    after = hop(own, along, -1)
    far_low = hop(before[:half], along, 1)
    far_high = hop(after[half:], along, -1)
    return before, after, far_low, far_high


def torus_gather(rows, first, second):
    line = ring_gather(rows, first)
    own = ring_gather(rows, second)
    rest = jnp.concatenate(line, axis=0)
    return (rows, rest) + own + ring_gather(rest, second)


def z_gather(piece):
    half = piece.shape[0] // 2
    before = shift(piece, 1)
    after = shift(piece, -1)
    low, high = before[:half], after[half:]
    far = [shift(low, 1), shift(high, -1)]
    pieces = [piece, before, after] + far
    return pieces + [swap(p) for p in pieces]


def add(*terms):
    return sum(t.astype(F32) for t in terms).astype(BF16)


def ring_scatter(own, back, ahead, far, along):
    half = own.shape[0] // 2
    from_back = hop(far[:half], along, 1)
    from_ahead = hop(far[half:], along, -1)
    ahead = jnp.concatenate([add(ahead[:half], from_back), ahead[half:]], axis=0)
    back = jnp.concatenate([back[:half], add(back[half:], from_ahead)], axis=0)
    up = hop(ahead, along, 1)
    down = hop(back, along, -1)
    return add(own, up, down)


def torus_scatter(parts, first, second):
    own, back, ahead, far = [(parts[2 * i], parts[2 * i + 1]) for i in range(4)]
    from_back = hop(far[0], first, 1)
    from_ahead = hop(far[1], first, -1)
    plain_up = hop(ahead[1], first, 1)
    plain_down = hop(back[0], first, -1)
    down = [None, None]
    up = [None, None]
    for i in (1, 0):
        down[i] = hop(add(back[1][i], from_ahead[i]), first, -1)
        up[i] = hop(add(ahead[0][i], from_back[i]), first, 1)
    sums = [add(own[0][i], up[i], plain_down[i]) for i in (0, 1)]
    sums += [add(own[1][i], plain_up[i], down[i]) for i in (0, 1)]
    return ring_scatter(*sums, second)


def small_gather(value):
    for along in ("x", "y"):
        value = jnp.concatenate([value, hop(value, along, 1)], axis=0)
        value = jnp.concatenate([value, hop(value, along, 2)], axis=0)
    return value


def block_pieces(refs, outer, inner):
    count = refs[0].shape[0]
    half = count // 2
    start = (inner - 1) * count
    if outer < 3:
        if inner == 0:
            return [((refs[0], refs[2], refs[3])[outer], 0, count)]
        ref = (refs[1], refs[6], refs[7])[outer]
        return [(ref.at[pl.ds(start, count)], 0, count)]
    if inner == 0:
        return [(refs[4], 0, half), (refs[5], half, half)]
    if inner == 1:
        return [(refs[8].at[pl.ds(0, count)], 0, count)]
    if inner == 3:
        return [(refs[9].at[pl.ds(half, count)], 0, count)]
    return [(refs[8].at[pl.ds(count, half)], 0, half), (refs[9].at[pl.ds(0, half)], half, half)]


def block_copies(refs, quad, slot, buf, sems, turned):
    out = []
    for n, y, x in quad_owners(quad):
        for ref, at, rows in block_pieces(refs, *((x, y) if turned else (y, x))):
            dst = buf.at[slot, n, pl.ds(at, rows)]
            out.append(pltpu.make_async_copy(ref, dst, sems.at[slot]))
    return out


def quad_owners(q):
    qy, qx = QUADS[q]
    return [(2 * y + x, 2 * qy + y, 2 * qx + x) for y in range(2) for x in range(2)]


def weight_copies(pos_ref, refs, buf, sems):
    me = pos_ref[0]
    core = lax.rem(me, 2)
    width = refs[0].shape[1]
    out = [[] for _ in range(buf.shape[0])]
    for n, ref in enumerate(refs):
        k = n % 5
        chip = lax.rem(lax.div(me, 2) + (0, 3, 1, 2, 2)[k], 4)
        at = 2 * chip + (core if n < 5 else 1 - core)
        count = ref.shape[0]
        for i in range(count):
            j = i + (count if k == 4 else 0)
            dst = buf.at[j, pl.ds(pl.multiple_of(at * width, width), width)]
            out[j].append(pltpu.make_async_copy(ref.at[i], dst, sems.at[j]))
    return out


def pick_kernel(row_ref, rowt_ref, gate_ref, pick_ref, pickt_ref, rowgate_ref):
    rows, tokens = pick_ref.shape[1:]
    per = rows // 4
    top = row_ref.shape[1]

    def pair(p, carry):
        at = pl.ds(pl.multiple_of(lax.rem(p, 2) * per, 8), per)
        down = lax.broadcasted_iota(jnp.int32, (rows, tokens), 0)
        hits = jnp.zeros((rows, tokens), F32)
        gates = jnp.zeros((rows, tokens), F32)
        for k in range(top):
            same = down == row_ref[p, k : k + 1, :]
            hits = jnp.where(same, 1.0, hits)
            gates = jnp.where(same, gate_ref[p, k : k + 1, :], gates)
        pick_ref[p] = hits.astype(BF16)
        sums = jnp.sum(gates, axis=1, keepdims=True)
        for j in range(4):
            rowgate_ref[lax.div(p, 2), j, at] = jnp.broadcast_to(
                sums[j * per : (j + 1) * per], (per, 128)
            )
        across = lax.broadcasted_iota(jnp.int32, (tokens, rows), 1)
        hits = jnp.zeros((tokens, rows), F32)
        for k in range(top):
            hits = jnp.where(across == rowt_ref[p, :, k : k + 1], 1.0, hits)
        pickt_ref[p] = hits.astype(BF16)
        return carry

    lax.fori_loop(0, pick_ref.shape[0], pair, 0)


def columns(width, step, tile=TILE):
    def run(c, carry):
        step(pl.ds(pl.multiple_of(c * tile, tile), tile))
        return carry

    lax.fori_loop(0, width // tile, run, 0)


def combine_quad(q, pickt_ref, rows_buf, buf):
    per = rows_buf.shape[1] // 2

    def combine(at):
        for i in range(2):
            rows = rows_buf[:, i * per : (i + 1) * per, at].reshape(-1, TILE)
            sums = jnp.dot(pickt_ref[2 * q + i], rows, preferred_element_type=F32)
            buf[2 * i : 2 * i + 2, :, at] = sums.astype(BF16).reshape(2, -1, TILE)

    columns(buf.shape[-1], combine)


def part_copies(q, buf, refs, turned, sems):
    out = []
    for n, y, x in quad_owners(q):
        outer, inner = (x, y) if turned else (y, x)
        ref = refs[2 * (outer % 2) + inner // 2].at[inner % 2]
        out.append(pltpu.make_async_copy(buf.at[n], ref, sems.at[n]))
    return out


def experts_kernel(pos_ref, pick_ref, pickt_ref, rowgate_ref, *refs):
    token_refs, cot_refs, weight_refs = refs[:10], refs[10:20], refs[20:30]
    mixed_refs, grad_refs, kept_rows_ref, kept_grads_ref = refs[30:34], refs[34:38], refs[38], refs[39]
    tokens, cots, token_rows, cot_rows, weight, grad = refs[40:46]
    token_sems, cot_sems, weight_sems, out_sems, kept_sems = refs[46:]
    width = weight.shape[1]
    hid = weight.shape[2] // 3
    per = token_rows.shape[2] // 2
    nt = (((1,), (1,)), ((), ()))
    weights = weight_copies(pos_ref, weight_refs, weight, weight_sems)
    for q in range(4):
        for c in block_copies(token_refs, q, q, tokens, token_sems, False):
            c.start()
    for q in range(4):
        for c in block_copies(cot_refs, q, q, cots, cot_sems, True):
            c.start()

    def gather_all(buf, rows_buf, sems):
        def gather_quad(q, carry):
            pltpu.make_async_copy(buf.at[q], buf.at[q], sems.at[q]).wait()

            def gather(at):
                for i in range(2):
                    values = buf[q, 2 * i : 2 * i + 2, :, at].reshape(-1, TILE)
                    rows = jnp.dot(pick_ref[2 * q + i], values, preferred_element_type=F32)
                    rows = rows.astype(BF16).reshape(4, per, TILE)
                    rows_buf[q, :, i * per : (i + 1) * per, at] = rows

            columns(width, gather)
            return carry

        lax.fori_loop(0, 4, gather_quad, 0)

    for c in weights[0]:
        c.start()
    gather_all(tokens, token_rows, token_sems)
    for copies in weights[1:]:
        for c in copies:
            c.start()
    gather_all(cots, cot_rows, cot_sems)

    def expert(j, carry):
        pltpu.make_async_copy(weight.at[j], weight.at[j], weight_sems.at[j]).wait()
        rows = grad.shape[0]
        pre = jnp.dot(
            token_rows[:, j].reshape(rows, width),
            weight[j, :, : 2 * hid],
            preferred_element_type=F32,
        )
        back = jnp.dot(
            cot_rows[:, j].reshape(rows, width),
            weight[j, :, 2 * hid :],
            preferred_element_type=F32,
        )
        gate = rowgate_ref[:, j].reshape(rows, 128)[:, :1]
        g, u = pre[:, :hid], pre[:, hid:]
        s = 1.0 / (1.0 + jnp.exp(-g))
        back = back * gate
        grad[:, :hid] = (back * u * s * (1.0 + g * (1.0 - s))).astype(BF16)
        grad[:, hid : 2 * hid] = (back * (g * s)).astype(BF16)
        grad[:, 2 * hid :] = (gate * (g * s) * u).astype(BF16)

        def outs(at):
            out = lax.dot_general(
                grad[:, 2 * hid :], weight[j, at, 2 * hid :], nt, preferred_element_type=F32
            )
            token_rows[:, j, :, at] = out.astype(BF16).reshape(4, -1, 2 * TILE)
            out = lax.dot_general(
                grad[:, : 2 * hid], weight[j, at, : 2 * hid], nt, preferred_element_type=F32
            )
            cot_rows[:, j, :, at] = out.astype(BF16).reshape(4, -1, 2 * TILE)

        columns(width, outs, 2 * TILE)
        return carry

    lax.fori_loop(0, 4, expert, 0)
    copies = []
    for side, (buf, rows_buf, refs) in enumerate(
        ((tokens, token_rows, mixed_refs), (cots, cot_rows, grad_refs))
    ):


        def combine(n, carry, side=side, buf=buf, rows_buf=rows_buf):
            q = 1 + 2 * n if side else 2 + n
            combine_quad(q, pickt_ref, rows_buf.at[q], buf.at[q])
            return carry

        lax.fori_loop(0, 2, combine, 0)
        for q in GIVE_FIRST[side]:
            some = part_copies(q, buf.at[q], refs, bool(side), out_sems.at[side, q])
            for c in some:
                c.start()
            copies += some
    for side, (rows_buf, kept_ref) in enumerate(
        ((token_rows, kept_rows_ref), (cot_rows, kept_grads_ref))
    ):
        for n, q in enumerate(GIVE_LATER[side]):
            c = pltpu.make_async_copy(rows_buf.at[q], kept_ref.at[n], kept_sems.at[side, n])
            c.start()
            copies.append(c)
    for c in copies:
        c.wait()


def later_kernel(pickt_ref, kept_rows_ref, kept_grads_ref, *refs):
    mixed_refs, grad_refs, rows_buf, buf, in_sems, out_sems = refs[:4], refs[4:8], *refs[8:]
    loads = []
    for side, kept_ref in enumerate((kept_rows_ref, kept_grads_ref)):
        for n in range(2):
            c = pltpu.make_async_copy(kept_ref.at[n], rows_buf.at[side, n], in_sems.at[side, n])
            c.start()
            loads.append(c)
    for c in loads:
        c.wait()

    def combine(m, carry):
        side, n = lax.div(m, 2), lax.rem(m, 2)
        combine_quad(n * (1 + side), pickt_ref, rows_buf.at[side, n], buf.at[side, n])
        return carry

    lax.fori_loop(0, 4, combine, 0)
    copies = []
    for side, refs in enumerate((mixed_refs, grad_refs)):
        for n, q in enumerate(GIVE_LATER[side]):
            copies += part_copies(q, buf.at[side, n], refs, bool(side), out_sems.at[side, n])
    for c in copies:
        c.start()
    for c in copies:
        c.wait()


def cost(flops, moved):
    return pl.CostEstimate(flops=flops, bytes_accessed=moved, transcendentals=0)


GIVE_FIRST = ((2, 3), (1, 3))
GIVE_LATER = ((0, 1), (0, 2))
PARAMS = pltpu.CompilerParams(vmem_limit_bytes=60 * 1024 * 1024)
DMA = pltpu.SemaphoreType.DMA


def body(tokens, cotangent, expert_ids, slot_ids, gate_weights, w_gate_up, w_down):
    tok_count, width = tokens.shape
    top = expert_ids.shape[1]
    experts = w_gate_up.shape[0]
    hid = w_down.shape[1]
    group = lax.axis_size("expert")
    capacity = 5 * tok_count * top // (4 * experts * group)
    local_rows = experts * capacity
    pair_tokens = 2 * tok_count
    pair_rows = 2 * local_rows
    sds = jax.ShapeDtypeStruct

    places = (expert_ids * capacity + slot_ids).astype(F32).T
    info = small_gather(jnp.concatenate([places, gate_weights.T], axis=0)[None])
    info = info.reshape(4, 4, 2 * top, tok_count)
    info = jnp.stack([info[0], info[1], info[3], info[2]])
    info = jnp.stack([info[:, 0], info[:, 1], info[:, 3], info[:, 2]], axis=1)
    info = info.reshape(2, 2, 2, 2, 2 * top, tok_count)
    owner = jnp.arange(2)[None, None, None, :, None, None]
    place = info[:, :, :, :, :top].astype(jnp.int32) - lax.axis_index("expert") * local_rows
    mine = (place >= 0) & (place < local_rows)
    row = place // capacity * (2 * capacity) + owner * capacity + place % capacity
    row = jnp.where(mine, row, -1)
    by_pair = lambda v: v.transpose(0, 2, 1, 4, 3, 5).reshape(8, top, pair_tokens)
    row = by_pair(row)
    gates = by_pair(info[:, :, :, :, top:])
    picks = pl.pallas_call(
        pick_kernel,
        out_shape=(
            sds((8, pair_rows, pair_tokens), BF16),
            sds((8, pair_tokens, pair_rows), BF16),
            sds((4, experts, 4 * capacity, 128), F32),
        ),
        in_specs=[VMEM] * 3,
        out_specs=(VMEM,) * 3,
        compiler_params=PARAMS,
        cost_estimate=cost(0, 8 << 20),
    )
    pick, pickt, rowgate = picks(row, jnp.swapaxes(row, 1, 2), gates)

    pos = lax.axis_index("dp").astype(jnp.int32).reshape(1)
    weights = z_gather(jnp.concatenate([w_gate_up, jnp.swapaxes(w_down, 1, 2)], axis=2))
    part = sds((2, tok_count, width), BF16)
    kept = sds((2, experts, 4 * capacity, width), BF16)
    token_buf = pltpu.VMEM((4, 4, tok_count, width), BF16)
    row_buf = pltpu.VMEM((4, experts, 4 * capacity, width), BF16)
    through = pl.pallas_call(
        experts_kernel,
        out_shape=(part,) * 8 + (kept, kept),
        in_specs=[SMEM] + [VMEM] * 3 + [ANY] * 30,
        out_specs=(ANY,) * 10,
        scratch_shapes=[
            token_buf,
            token_buf,
            row_buf,
            row_buf,
            pltpu.VMEM((experts, width, 3 * hid), BF16),
            pltpu.VMEM((16 * capacity, 3 * hid), BF16),
            DMA((4,)),
            DMA((4,)),
            DMA((experts,)),
            DMA((2, 4, 4)),
            DMA((2, 2)),
        ],
        compiler_params=PARAMS,
        cost_estimate=cost(20 * 10**9, 60 << 20),
    )
    done = through(
        pos,
        pick,
        pickt,
        rowgate,
        *torus_gather(tokens, "x", "y"),
        *torus_gather(cotangent, "y", "x"),
        *weights,
    )
    later = pl.pallas_call(
        later_kernel,
        out_shape=(part,) * 8,
        in_specs=[VMEM, ANY, ANY],
        out_specs=(ANY,) * 8,
        scratch_shapes=[
            pltpu.VMEM((2, 2, experts, 4 * capacity, width), BF16),
            pltpu.VMEM((2, 2, 4, tok_count, width), BF16),
            DMA((2, 2)),
            DMA((2, 2, 4)),
        ],
        compiler_params=PARAMS,
        cost_estimate=cost(3 * 10**9, 15 << 20),
    )
    rest = later(pickt, done[8], done[9])
    mixed = torus_scatter(rest[:4] + done[:4], "y", "x")
    grads = torus_scatter(rest[4:] + done[4:8], "x", "y")
    return (mixed, grads)


def solution(mesh):
    rows = P(("dp", "expert"), None)
    placed = (rows, rows, rows, rows, rows, P("expert", "dp", None), P("expert", None, "dp"))

    return jax.shard_map(body, mesh=mesh, in_specs=placed, out_specs=(rows, rows), check_vma=False)
```
